256 devices in a mesh: ep: 64 (over z, y, core), sp: 4 (over x).
Axes of the slice: x: 4, y: 4, z: 8, core: 2. Of those that a mesh axis runs over, the one named last changes fastest.
Arguments:
- stream: bfloat16 [32768, 4096], P(('ep', 'sp')), may hold values from -30 to 30
- query_base: bfloat16 [32768, 4096], P(('ep', 'sp')), may hold values from -40 to 40
- key_heads: bfloat16 [32768, 1024], P(('ep', 'sp')), may hold values from -6 to 6
- value_heads: bfloat16 [32768, 1024], P(('ep', 'sp')), may hold values from -12 to 12
- attention_gain: bfloat16 [4096], replicated, may hold values from 0.099609375 to 1.8984375
- expert_gain: bfloat16 [4096], replicated, may hold values from 0.099609375 to 1.8984375
- adapter_down: bfloat16 [4096, 128], P('sp'), may hold values from -0.09375 to 0.09375
- adapter_up: bfloat16 [4096, 128], P('sp'), may hold values from -1 to 1
- user_index: int32 [64], P('ep'), may hold values from 0 to 3
- routes: int32 [32768, 2], P('ep'), may hold values from 0 to 63, all different within a row; in each aligned block of 128 rows (0 to 127, 128 to 255, ...) at most 5 rows name the same one
- route_weights: int32 [32768, 2], P(('ep', 'sp')), may hold values from 1 to 4
- gate_weight: bfloat16 [64, 4096, 1536], P('ep', None, 'sp'), may hold values from -0.09375 to 0.09375
- up_weight: bfloat16 [64, 4096, 1536], P('ep', None, 'sp'), may hold values from -0.09375 to 0.09375
- down_weight: bfloat16 [64, 1536, 4096], P('ep', 'sp'), may hold values from -0.15625 to 0.15625
Outputs:
- hidden_state: bfloat16 [32768, 4096], P(('ep', 'sp'))
- moe_out: bfloat16 [32768, 4096], P(('ep', 'sp'))
The draws below stay inside these ranges and needn't reach their ends.
Inputs may be any that keep to these rules, and one draw needn't show every extreme that they name: `routes`: each row names 2 different experts. In each aligned block of 128 rows (the tokens of one device) no expert is named more than 5 times, and in some block some expert is named exactly 5 times.
All inputs are finite; a program needn't handle non-finite values.
Results may differ from the reference program's by a relative error of at most 0.019.
Values may be sent and summed in bfloat16 or wider, within the bound.
No kernel may reach another device: no remote copies, remote signals or barrier semaphores. Data moves between devices by JAX's collectives and lax.ppermute only.
A program may use at most 128 MiB of HBM per device.

```python
import math
import jax
import jax.numpy as jnp
import numpy as np
from jax import lax

D = 4096
HEADS = 32
KV_HEADS = 8
HEAD = 128
FF = 1536
USERS = 4
RANK = 32
TOP = 2
TOK_DEV = 128
SEQ_LEN = 512
SEQS = 64
TOKENS = 32768
EXPERTS = 64
CAP = 5
N_SP = 4


def key_field(key):
    base_key = jax.random.fold_in(key, 101)
    field_rows = jnp.clip(jax.random.normal(base_key, (TOKENS, KV_HEADS * HEAD), jnp.float32), -6.0, 6.0)
    return field_rows


def draw_key_heads(key, part):
    return key_field(key).astype(jnp.bfloat16)


def draw_query_base(key, part):
    base_key = jax.random.fold_in(key, 201)
    base_rows = jnp.clip(jax.random.normal(base_key, (TOKENS, D), jnp.float32), -6.0, 6.0)
    return base_rows.astype(jnp.bfloat16)


def draw_stream(key, part):
    base_key = jax.random.fold_in(key, 301)
    field_rows = jnp.clip(jax.random.normal(base_key, (TOKENS, D), jnp.float32), -6.0, 6.0)
    return field_rows.astype(jnp.bfloat16)


def set_ends(array, stream_key, low, high):
    shape = array.shape
    index_at = [jax.random.randint(jax.random.fold_in(stream_key, axis), (), 0, shape[axis]) for axis in range(len(shape))]
    array = array.at[tuple(index_at)].set(low)
    longest = shape.index(max(shape))
    index_at[longest] = (index_at[longest] + 1) % shape[longest]
    return array.at[tuple(index_at)].set(high)


def shard_levels(key, shape, split, smallest, top_value):
    factor_of, own = 1.0, jax.random.fold_in(key, 6)
    for dim, blocks in split:
        heights = jnp.exp(jax.random.uniform(jax.random.fold_in(own, dim), (blocks,), jnp.float32, smallest / len(split), top_value / len(split)))
        factor_of = factor_of * jnp.repeat(heights, shape[dim] // blocks).reshape([-1 if axis == dim else 1 for axis in range(len(shape))])
    return factor_of


def assign_block(own_key, own, number, rows, amount, top, most, skew):
    ranking = jax.random.permutation(own_key, amount)
    crowded, usual = portions_of(amount, rows * top, most, skew, True), portions_of(amount, rows * top, most, skew, False)
    places = jnp.arange(amount)

    def named(sizes, turn):
        used = int((sizes > 0).sum())
        fixed = max(1, used // 4)
        passed = fixed + (places - fixed + turn * (used - fixed)) % max(1, amount - fixed)
        return jnp.zeros((amount,), jnp.int32).at[ranking[jnp.where(places < fixed, places, passed)]].set(jnp.asarray(sizes, jnp.int32))

    sizes = jnp.where(number % 4 == 0, named(crowded, number // 4), named(usual, number - number // 4 - 1))
    mixed = jax.random.permutation(jax.random.fold_in(own, 3), amount)
    donor, sink = mixed[0:amount // 2 * 2:2], mixed[1:amount // 2 * 2:2]
    room = jnp.minimum(sizes[donor] - 1, most - sizes[sink]) // 2
    room = jnp.where((donor == ranking[0]) | (sink == ranking[0]) | (sizes[sink] == 0), 0, jnp.maximum(room, 0))
    passed = jax.random.randint(jax.random.fold_in(own, 4), (amount // 2,), 0, 1 << 20) % (room + 1)
    sizes = sizes.at[donor].add(-passed).at[sink].add(passed)
    members = jnp.searchsorted(jnp.cumsum(sizes), jnp.arange(rows * top), side="right").astype(jnp.int32)
    grid = members.reshape(top, rows).T
    grid = grid[jax.random.permutation(jax.random.fold_in(own, 1), rows)]
    turn = jax.random.randint(jax.random.fold_in(own, 2), (rows, 1), 0, top)
    return jnp.take_along_axis(grid, (jnp.arange(top)[None, :] + turn) % top, axis=1)


def portions_of(amount, total, most, slope, full):
    weights = [(1 << 20) // math.isqrt(rank ** slope) + 1 for rank in range(1, amount + 1)]
    largest = most if full else min(most, max(-(-total // amount), total * weights[0] // sum(weights)))
    least = 1 if total - largest >= amount - 1 else 0
    holding, spare = [largest] + [least] * (amount - 1), total - largest - least * (amount - 1)
    while spare > 0:
        free = [i for i in range(1, amount) if holding[i] < largest] or [i for i in range(1, amount) if holding[i] < most]
        whole, left = sum([weights[i] for i in free]), spare
        for i in free:
            more = min(most - holding[i], max(1, left * weights[i] // whole), spare)
            holding[i] = holding[i] + more
            spare = spare - more
    return np.array(holding)


def scatter_about(rng, shape, deviation, most, pieces=(), held_as=jnp.bfloat16):
    factor_of = shard_levels(rng, shape, pieces, -0.22, 0.18) if pieces else 1.0
    entries = jax.random.normal(rng, shape, jnp.float32) * deviation * factor_of
    return jnp.minimum(jnp.maximum(entries, -most), most).astype(held_as)


def setup_inputs(seed: int = 0) -> dict:
    streams_of = jax.random.split(jax.random.key(seed), 15)
    stream = draw_stream(jax.random.fold_in(streams_of[14], 71), 0)
    query_base = draw_query_base(jax.random.fold_in(streams_of[14], 71), 0)
    key_heads = draw_key_heads(jax.random.fold_in(streams_of[14], 71), 0)
    value_heads = scatter_about(streams_of[3], (TOKENS, KV_HEADS * HEAD), 2.0, 12.0, ((0, 256),))
    attention_gain = jnp.clip(1.0 + 0.18 * jax.random.normal(streams_of[4], (D,), jnp.float32), 0.099609375, 1.8984375).astype(jnp.bfloat16)
    expert_gain = jnp.clip(1.0 + 0.18 * jax.random.normal(streams_of[5], (D,), jnp.float32), 0.099609375, 1.8984375).astype(jnp.bfloat16)
    adapter_down = scatter_about(streams_of[6], (D, USERS * RANK), D ** -0.5, 0.09375, ((0, 4),))
    adapter_up = scatter_about(streams_of[7], (D, USERS * RANK), RANK ** -0.5, 1.0, ((0, 4),))
    user_index = set_ends(jax.random.randint(streams_of[8], (SEQS,), 0, USERS), jax.random.fold_in(streams_of[8], 1), 0, USERS - 1).astype(jnp.int32)
    routes_keys = jax.random.split(jax.random.fold_in(streams_of[9], 1), TOKENS // TOK_DEV)
    routes_turns = jax.random.permutation(jax.random.fold_in(streams_of[9], 3), TOKENS // TOK_DEV)
    routes = jax.vmap(lambda own, number: assign_block(jax.random.fold_in(streams_of[9], 2), own, number, TOK_DEV, EXPERTS, TOP, CAP, 2))(routes_keys, routes_turns).reshape((TOKENS, TOP))
    route_weights = set_ends(jax.random.randint(streams_of[10], (TOKENS, TOP), 1, 5), jax.random.fold_in(streams_of[10], 1), 1, 4).astype(jnp.int32)
    gate_weight = scatter_about(streams_of[11], (EXPERTS, D, FF), D ** -0.5, 0.09375, ((0, 64), (2, 4)))
    up_weight = scatter_about(streams_of[12], (EXPERTS, D, FF), D ** -0.5, 0.09375, ((0, 64), (2, 4)))
    down_weight = scatter_about(streams_of[13], (EXPERTS, FF, D), FF ** -0.5, 0.15625, ((0, 64), (1, 4)))
    return dict(stream=stream, query_base=query_base, key_heads=key_heads, value_heads=value_heads, attention_gain=attention_gain, expert_gain=expert_gain, adapter_down=adapter_down, adapter_up=adapter_up, user_index=user_index, routes=routes, route_weights=route_weights, gate_weight=gate_weight, up_weight=up_weight, down_weight=down_weight)


epsilon = 1e-06

def rms_scale(inputs, gain_vec):
    widened = inputs.astype(jnp.float32)
    return widened * lax.rsqrt(lax.optimization_barrier(jnp.mean(widened * widened, axis=-1, keepdims=True)) + epsilon) * gain_vec.astype(jnp.float32)

def route_slots(block_routes, experts):
    flat_routes = block_routes.reshape(-1)
    matches = (flat_routes[:, None] == jnp.arange(experts, dtype=jnp.int32)[None, :]).astype(jnp.int32)
    earlier = jnp.cumsum(matches, axis=0) - matches
    return (flat_routes, lax.optimization_barrier(jnp.sum(earlier * matches, axis=1)).astype(jnp.int32))

def attention_block(stream_rows, base_rows, key_rows, value_rows, user_id, attention_gain, adapter_down, adapter_up):
    normed = rms_scale(stream_rows, attention_gain).astype(jnp.bfloat16)
    down_cols = lax.dynamic_slice_in_dim(adapter_down, (user_id * RANK).astype(jnp.int32), RANK, 1)
    up_cols = lax.dynamic_slice_in_dim(adapter_up, (user_id * RANK).astype(jnp.int32), RANK, 1)
    low_rank = jnp.dot(normed, down_cols, preferred_element_type=jnp.float32).astype(jnp.bfloat16)
    adapter_delta = jnp.dot(low_rank, up_cols.T, preferred_element_type=jnp.float32)
    queries = (base_rows.astype(jnp.float32) + adapter_delta).astype(jnp.bfloat16)
    group_size = HEADS // KV_HEADS
    row_total = queries.shape[0]
    query_heads = queries.reshape(row_total, KV_HEADS, group_size, HEAD).astype(jnp.float32)
    key_split = key_rows.reshape(-1, KV_HEADS, HEAD).astype(jnp.float32)
    value_split = value_rows.reshape(-1, KV_HEADS, HEAD).astype(jnp.float32)
    scores = jnp.einsum('qhgd,khd->hgqk', query_heads, key_split) * HEAD ** (-0.5)
    row_max = lax.optimization_barrier(jnp.max(scores, axis=-1, keepdims=True))
    exponent = jnp.exp(scores - row_max)
    attn_probs = (exponent / lax.optimization_barrier(jnp.sum(exponent, axis=-1, keepdims=True))).astype(jnp.bfloat16)
    attended = jnp.einsum('hgqk,khd->qhgd', attn_probs.astype(jnp.float32), value_split).reshape(row_total, D)
    return (stream_rows.astype(jnp.float32) + attended).astype(jnp.bfloat16)

def reference(stream, query_base, key_heads, value_heads, attention_gain, expert_gain, adapter_down, adapter_up, user_index, routes, route_weights, gate_weight, up_weight, down_weight):

    def per_sequence(packed):
        stream_rows, base_rows, key_rows, value_rows, user_id = packed
        return attention_block(stream_rows, base_rows, key_rows, value_rows, user_id, attention_gain, adapter_down, adapter_up)
    hidden_state = lax.map(per_sequence, (stream.reshape(SEQS, SEQ_LEN, D), query_base.reshape(SEQS, SEQ_LEN, D), key_heads.reshape(SEQS, SEQ_LEN, -1), value_heads.reshape(SEQS, SEQ_LEN, -1), user_index)).reshape(TOKENS, D)
    normed_moe = rms_scale(hidden_state, expert_gain).astype(jnp.bfloat16)
    weights = route_weights.astype(jnp.float32)
    weights = weights / lax.optimization_barrier(jnp.sum(weights, axis=1, keepdims=True))
    blocks = TOKENS // TOK_DEV
    flat_all, slot_all = jax.vmap(lambda block_rows: route_slots(block_rows, EXPERTS))(routes.reshape(blocks, TOK_DEV, TOP))
    block_ids = jnp.broadcast_to(jnp.arange(blocks, dtype=jnp.int32)[:, None], flat_all.shape)
    token_ids = block_ids * TOK_DEV + jnp.arange(TOK_DEV * TOP, dtype=jnp.int32)[None, :] // TOP
    slot_table = jnp.full((EXPERTS, blocks, CAP), TOKENS, jnp.int32).at[flat_all, block_ids, slot_all].set(token_ids)
    share_table = jnp.zeros((EXPERTS, blocks, CAP), jnp.float32).at[flat_all, block_ids, slot_all].set(weights.reshape(blocks, -1))
    padded = jnp.concatenate([normed_moe, jnp.zeros((1, D), jnp.bfloat16)], axis=0)

    def expert_step(total, packed):
        index_rows, share_rows, gate_one, up_one, down_one = packed
        rows_in = padded[index_rows]
        gate_out = jnp.dot(rows_in, gate_one, preferred_element_type=jnp.float32)
        up_out = jnp.dot(rows_in, up_one, preferred_element_type=jnp.float32)
        activated = (jax.nn.silu(gate_out) * up_out).astype(jnp.bfloat16)
        parts = jnp.einsum('mjf,jfd->jmd', activated.reshape(-1, N_SP, FF // N_SP).astype(jnp.float32), down_one.reshape(N_SP, FF // N_SP, D).astype(jnp.float32)).astype(jnp.bfloat16)
        expert_out = lax.optimization_barrier(jnp.sum(parts.astype(jnp.float32), axis=0)).astype(jnp.bfloat16)
        total = total.at[index_rows].add(share_rows[:, None] * expert_out.astype(jnp.float32))
        return (total, None)
    total, unused = lax.scan(expert_step, jnp.zeros((TOKENS + 1, D), jnp.float32), (slot_table.reshape(EXPERTS, -1), share_table.reshape(EXPERTS, -1), gate_weight, up_weight, down_weight))
    moe_out = total[:TOKENS].astype(jnp.bfloat16)
    return (hidden_state, moe_out)
```

```python
import functools

import jax
import jax.numpy as jnp
from jax import lax
from jax.experimental import pallas as pl
from jax.experimental.pallas import tpu as pltpu
from jax.sharding import PartitionSpec as P

D = 4096
HEADS = 32
KV_HEADS = 8
HEAD = 128
RANK = 32
SLOTS = 5
SEG = 8
WIDE = D // SEG
EXPERTS = 64
CHUNKS = (1, 2, 2)

epsilon = 1e-06
bf16 = jnp.bfloat16
f32 = jnp.float32
VMEM_SPEC = pl.BlockSpec(memory_space=pltpu.VMEM)
SMEM_SPEC = pl.BlockSpec(memory_space=pltpu.SMEM)
PARAMS = pltpu.CompilerParams(vmem_limit_bytes=56 << 20)


def dot(a, b, contract=((1,), (0,))):
    return lax.dot_general(a, b, (contract, ((), ())), preferred_element_type=f32)


def one_hot_dot(a, b, contract=((1,), (0,))):
    return dot(a, b, contract).astype(bf16)


def iota(shape, dim):
    return lax.broadcasted_iota(jnp.int32, shape, dim)


def to_segments():
    n = EXPERTS * SEG
    r, q = iota((n, n), 0), iota((n, n), 1)
    return (q == (r & (SEG - 1)) * EXPERTS + (r >> 3)).astype(f32).astype(bf16)


def from_segments():
    n = EXPERTS * SEG
    q, r = iota((n, n), 0), iota((n, n), 1)
    return (r == (q & (EXPERTS - 1)) * SEG + (q >> 6)).astype(f32).astype(bf16)


def slot_masks(routes_ref, start, tokens):
    own = routes_ref[:, pl.ds(start, tokens)]
    e = iota((EXPERTS, tokens), 0)
    first = (own[0:1, :] == e).astype(f32)
    second = (own[1:2, :] == e).astype(f32)
    before = (iota((tokens, tokens), 0) < iota((tokens, tokens), 1)).astype(f32)
    count = dot((first + second).astype(bf16), before.astype(bf16))
    return first, second, count


def attention_kernel(user_ref, sp_ref, stream, base, *refs):
    keys, values, adapters = refs[0:4], refs[4:8], refs[8:12]
    gain_a, gain_e, routes = refs[12:15]
    n_out = 1 + len(CHUNKS)
    hidden = refs[15]
    sends = refs[16 : 15 + n_out]
    xn, query, stack = refs[15 + n_out :]
    tokens = stream.shape[0]
    me = sp_ref[0]

    total = jnp.zeros((tokens, 1), f32)
    for s in range(SEG):
        x = stream[:, s * WIDE : (s + 1) * WIDE].astype(f32)
        total += jnp.sum(x * x, axis=1, keepdims=True)
    scale = lax.rsqrt(total * (1.0 / D) + epsilon)
    for s in range(SEG):
        cols = slice(s * WIDE, (s + 1) * WIDE)
        xn[:, cols] = (
            stream[:, cols].astype(f32) * scale * gain_a[:, cols].astype(f32)
        ).astype(bf16)

    quarter = D // 4
    starts = [
        pl.multiple_of(((me + shift) & 3) * quarter, quarter) for shift in (0, 3, 1, 2)
    ]
    low = jnp.zeros((tokens, RANK), f32)
    for start, part in zip(starts, adapters):
        low += dot(xn[:, pl.ds(start, quarter)], part[0:RANK, :], ((1,), (1,)))
    low = low.astype(bf16)
    for start, part in zip(starts, adapters):
        cols = pl.ds(start, quarter)
        delta = dot(low, part[RANK : 2 * RANK, :])
        query[:, cols] = (base[:, cols].astype(f32) + delta).astype(bf16)

    group = HEADS // KV_HEADS
    total = jnp.zeros((tokens, 1), f32)
    for g in range(KV_HEADS):
        kv = slice(g * HEAD, (g + 1) * HEAD)
        q = jnp.concatenate(
            [query[:, (g * group + h) * HEAD : (g * group + h + 1) * HEAD] for h in range(group)],
            axis=0,
        )
        k = jnp.concatenate([r[:, kv] for r in keys], axis=0)
        v = jnp.concatenate([r[:, kv] for r in values], axis=0)
        scores = dot(q, k, ((1,), (1,))) * HEAD ** (-0.5)
        e = jnp.exp(scores - jnp.max(scores, axis=1, keepdims=True))
        p = (e * (1.0 / jnp.sum(e, axis=1, keepdims=True))).astype(bf16)
        o = dot(p, v)
        for h in range(group):
            cols = slice((g * group + h) * HEAD, (g * group + h + 1) * HEAD)
            state = (
                stream[:, cols].astype(f32) + o[h * tokens : (h + 1) * tokens, :]
            ).astype(bf16)
            hidden[:, cols] = state
            wide = state.astype(f32)
            total += jnp.sum(wide * wide, axis=1, keepdims=True)

    scale = lax.rsqrt(total * (1.0 / D) + epsilon)
    first, second, count = slot_masks(routes, pl.multiple_of(me * tokens, tokens), tokens)
    named = first + second
    pick = jnp.concatenate(
        [jnp.where(count == c, named, 0.0) for c in range(SLOTS)], axis=0
    ).astype(bf16)
    for s in range(SEG):
        cols = slice(s * WIDE, (s + 1) * WIDE)
        hn = (hidden[:, cols].astype(f32) * scale * gain_e[:, cols].astype(f32)).astype(bf16)
        rows = one_hot_dot(pick, hn)
        for c in range(SLOTS):
            stack[s * EXPERTS : (s + 1) * EXPERTS, c * WIDE : (c + 1) * WIDE] = rows[
                c * EXPERTS : (c + 1) * EXPERTS, :
            ]
    order = to_segments()
    c = 0
    for n, send in zip(CHUNKS, sends):
        send[...] = one_hot_dot(order, stack[:, c * WIDE : (c + n) * WIDE])
        c += n


def attention(user, sp, stream, base, keys, values, adapters, gain_a, gain_e, routes):
    tokens = stream.shape[0]
    outs = [jax.ShapeDtypeStruct((tokens, D), bf16)] + [
        jax.ShapeDtypeStruct((EXPERTS * SEG, n * WIDE), bf16) for n in CHUNKS
    ]
    return pl.pallas_call(
        attention_kernel,
        out_shape=outs,
        in_specs=[SMEM_SPEC] * 2 + [VMEM_SPEC] * 17,
        out_specs=[VMEM_SPEC] * len(outs),
        scratch_shapes=[
            pltpu.VMEM((tokens, D), bf16),
            pltpu.VMEM((tokens, D), bf16),
            pltpu.VMEM((EXPERTS * SEG, SLOTS * WIDE), bf16),
        ],
        compiler_params=PARAMS,
        name="attention",
    )(user, sp, stream, base, *keys, *values, *adapters, gain_a, gain_e, routes)


def blocks_of(n):
    half = n * EXPERTS // 2
    for c in range(n):
        lo, hi = c * EXPERTS, (c + 1) * EXPERTS
        for which, (a, b) in enumerate(((0, half), (half, 2 * half))):
            x, y = max(lo, a), min(hi, b)
            if x < y:
                yield c, which, x - a, x - lo, y - x


def arrive_kernel(n, received, *halves):
    rows = one_hot_dot(from_segments(), received[...])
    for c, which, to, at, size in blocks_of(n):
        for s in range(SEG):
            halves[which][to : to + size, s * WIDE : (s + 1) * WIDE] = rows[
                s * EXPERTS + at : s * EXPERTS + at + size, c * WIDE : (c + 1) * WIDE
            ]


def arrive(n, received):
    half = jax.ShapeDtypeStruct((n * EXPERTS // 2, D), bf16)
    return pl.pallas_call(
        functools.partial(arrive_kernel, n),
        out_shape=[half, half],
        in_specs=[VMEM_SPEC],
        out_specs=[VMEM_SPEC] * 2,
        compiler_params=PARAMS,
        name="arrive",
    )(received)


def leave_kernel(n, *refs):
    terms, out, stack = (refs[0:3], refs[3:6]), refs[6], refs[7]
    for c, which, at, to, size in blocks_of(n):
        for s in range(SEG):
            cols = slice(s * WIDE, (s + 1) * WIDE)
            total = sum(t[at : at + size, cols].astype(f32) for t in terms[which])
            stack[
                s * EXPERTS + to : s * EXPERTS + to + size, c * WIDE : (c + 1) * WIDE
            ] = total.astype(bf16)
    out[...] = one_hot_dot(to_segments(), stack[...])


def leave(n, terms_a, terms_b):
    shape = (EXPERTS * SEG, n * WIDE)
    return pl.pallas_call(
        functools.partial(leave_kernel, n),
        out_shape=jax.ShapeDtypeStruct(shape, bf16),
        in_specs=[VMEM_SPEC] * 6,
        out_specs=VMEM_SPEC,
        scratch_shapes=[pltpu.VMEM(shape, bf16)],
        compiler_params=PARAMS,
        name="leave",
    )(*terms_a, *terms_b)


STEPS = 4


def expert_kernel(n, *refs):
    rows, (gate, up, down) = refs[0:n], refs[n : n + 3]
    outs = refs[n + 3 : 2 * n + 3]
    gate_sum, up_sum, act = refs[2 * n + 3 :]
    i = pl.program_id(0)
    depth = D // STEPS

    @pl.when(i == 0)
    def _():
        gate_sum[...] = jnp.zeros_like(gate_sum)
        up_sum[...] = jnp.zeros_like(up_sum)

    @pl.when(i < STEPS)
    def _():
        cols = pl.ds(pl.multiple_of(i * depth, depth), depth)
        x = jnp.concatenate([r[:, cols] for r in rows], axis=0)
        gate_sum[...] += dot(x, gate[...])
        up_sum[...] += dot(x, up[...])

    @pl.when(i == STEPS - 1)
    def _():
        v = gate_sum[...]
        act[...] = (v / (1.0 + jnp.exp(-v)) * up_sum[...]).astype(bf16)

    @pl.when(i >= STEPS)
    def _():
        part = dot(act[...], down[...]).astype(bf16)
        size = rows[0].shape[0]
        for k in range(n):
            outs[k][...] = part[k * size : (k + 1) * size, :]


def expert(pieces, gate, up, down):
    n, size, hidden = len(pieces), pieces[0].shape[0], gate.shape[1]
    depth = D // STEPS
    first = lambda i: (jnp.minimum(i, STEPS - 1), 0)
    last = lambda i: (0, jnp.maximum(i - STEPS, 0))
    flops = 6 * n * size * D * hidden
    return pl.pallas_call(
        functools.partial(expert_kernel, n),
        out_shape=[jax.ShapeDtypeStruct((size, D), bf16)] * n,
        grid=(2 * STEPS,),
        in_specs=[pl.BlockSpec((size, D), lambda i: (0, 0))] * n
        + [pl.BlockSpec((depth, hidden), first)] * 2
        + [pl.BlockSpec((hidden, depth), last)],
        out_specs=[pl.BlockSpec((size, depth), last)] * n,
        scratch_shapes=[
            pltpu.VMEM((n * size, hidden), f32),
            pltpu.VMEM((n * size, hidden), f32),
            pltpu.VMEM((n * size, hidden), bf16),
        ],
        compiler_params=PARAMS,
        cost_estimate=pl.CostEstimate(
            flops=flops,
            transcendentals=n * size * hidden,
            bytes_accessed=6 * D * hidden + 4 * n * size * D,
        ),
        name="expert",
    )(*pieces, gate, up, down)


def combine_kernel(sp_ref, routes, weights, *refs):
    received, out, stack = refs[: len(CHUNKS)], refs[-2], refs[-1]
    tokens = out.shape[0]
    first, second, count = slot_masks(routes, pl.multiple_of(sp_ref[0] * tokens, tokens), tokens)
    w = weights[...].astype(f32)
    w = w / jnp.sum(w, axis=0, keepdims=True)
    share = first * w[0:1, :] + second * w[1:2, :]
    share = jnp.concatenate(
        [jnp.where(count == c, share, 0.0) for c in range(SLOTS)], axis=0
    )
    high = share.astype(bf16)
    rest = (share - high.astype(f32)).astype(bf16)
    order = from_segments()
    c = 0
    for n, r in zip(CHUNKS, received):
        stack[:, c * WIDE : (c + n) * WIDE] = one_hot_dot(order, r[...])
        c += n
    for s in range(SEG):
        rows = jnp.concatenate(
            [
                stack[s * EXPERTS : (s + 1) * EXPERTS, k * WIDE : (k + 1) * WIDE]
                for k in range(SLOTS)
            ],
            axis=0,
        )
        both = dot(high, rows, ((0,), (0,))) + dot(rest, rows, ((0,), (0,)))
        out[:, s * WIDE : (s + 1) * WIDE] = both.astype(bf16)


def combine(sp, routes, weights, received, tokens):
    return pl.pallas_call(
        combine_kernel,
        out_shape=jax.ShapeDtypeStruct((tokens, D), bf16),
        in_specs=[SMEM_SPEC] + [VMEM_SPEC] * (2 + len(received)),
        out_specs=VMEM_SPEC,
        scratch_shapes=[pltpu.VMEM((EXPERTS * SEG, SLOTS * WIDE), bf16)],
        compiler_params=PARAMS,
        name="combine",
    )(sp, routes, weights, *received)


def right(x):
    return lax.ppermute(x, "sp", [(i, (i + 1) % 4) for i in range(4)])


def left(x):
    return lax.ppermute(x, "sp", [(i, (i + 3) % 4) for i in range(4)])


def exchange(x, n):
    cut = x.reshape(EXPERTS, SEG, n * WIDE)
    moved = lax.all_to_all(cut, "ep", split_axis=0, concat_axis=0, tiled=True)
    return moved.reshape(EXPERTS * SEG, n * WIDE)


def feed_forward(n, sent, gate, up, down):
    a, b = arrive(n, exchange(sent, n))
    a_left, a_right = right(a), left(a)
    b_left, b_right = right(b), left(b)
    a_far, b_far = right(a_left), left(b_right)
    pa_far, pb_far = expert([a_far, b_far], gate, up, down)
    a_in, b_in = right(pa_far), left(pb_far)
    pa_left, pb_left, pa_right, pb_right = expert(
        [a_left, b_left, a_right, b_right], gate, up, down
    )
    pa, pb = expert([a, b], gate, up, down)
    add = lambda x, y: (x.astype(f32) + y.astype(f32)).astype(bf16)
    a_from_left, b_from_left = right(add(pa_right, a_in)), right(pb_right)
    a_from_right, b_from_right = left(pa_left), left(add(pb_left, b_in))
    out = leave(n, (pa, a_from_left, a_from_right), (pb, b_from_left, b_from_right))
    return exchange(out, n)


def on_device(
    stream,
    query_base,
    key_heads,
    value_heads,
    attention_gain,
    expert_gain,
    adapter_down,
    adapter_up,
    user_index,
    routes,
    route_weights,
    gate_weight,
    up_weight,
    down_weight,
):
    sp = lax.axis_index("sp").astype(jnp.int32).reshape(1)
    columns = user_index[0] * RANK + jnp.arange(RANK, dtype=jnp.int32)
    select = (columns[:, None] == jnp.arange(4 * RANK, dtype=jnp.int32)[None, :]).astype(bf16)
    adapter = jnp.concatenate(
        [
            one_hot_dot(select, adapter_down, ((1,), (1,))),
            one_hot_dot(select, adapter_up, ((1,), (1,))),
        ],
        axis=0,
    )
    k_left, k_right = right(key_heads), left(key_heads)
    v_left, v_right = right(value_heads), left(value_heads)
    d_left, d_right = right(adapter), left(adapter)
    keys = (key_heads, k_left, k_right, right(k_left))
    values = (value_heads, v_left, v_right, left(v_right))
    adapters = (adapter, d_left, d_right, right(d_left))
    routes_t, weights_t = routes.T, route_weights.T
    hidden, *sends = attention(
        user_index,
        sp,
        stream,
        query_base,
        keys,
        values,
        adapters,
        attention_gain.reshape(1, D),
        expert_gain.reshape(1, D),
        routes_t,
    )
    gate, up, down = gate_weight[0], up_weight[0], down_weight[0]
    received = [feed_forward(n, x, gate, up, down) for n, x in zip(CHUNKS, sends)]
    moe_out = combine(sp, routes_t, weights_t, received, stream.shape[0])
    return (hidden, moe_out)


def solution(mesh):
    in_specs = (
        P(("ep", "sp"), None),
        P(("ep", "sp"), None),
        P(("ep", "sp"), None),
        P(("ep", "sp"), None),
        P(),
        P(),
        P("sp", None),
        P("sp", None),
        P("ep"),
        P("ep", None),
        P(("ep", "sp"), None),
        P("ep", None, "sp"),
        P("ep", None, "sp"),
        P("ep", "sp", None),
    )
    out_specs = (P(("ep", "sp"), None), P(("ep", "sp"), None))
    return jax.shard_map(
        on_device, mesh=mesh, in_specs=in_specs, out_specs=out_specs, check_vma=False
    )
```

```python
import functools

import jax
import jax.numpy as jnp
from jax import lax
from jax.experimental import pallas as pl
from jax.experimental.pallas import tpu as pltpu
from jax.sharding import PartitionSpec as P

D = 4096
HEADS = 32
KV_HEADS = 8
HEAD = 128
RANK = 32
SLOTS = 5
SEG = 8
WIDE = D // SEG
EXPERTS = 64
CHUNKS = (1, 2, 2)

epsilon = 1e-06
bf16 = jnp.bfloat16
f32 = jnp.float32
VMEM_SPEC = pl.BlockSpec(memory_space=pltpu.VMEM)
SMEM_SPEC = pl.BlockSpec(memory_space=pltpu.SMEM)
PARAMS = pltpu.CompilerParams(vmem_limit_bytes=56 << 20)


def dot(a, b, contract=((1,), (0,))):
    return lax.dot_general(a, b, (contract, ((), ())), preferred_element_type=f32)


def one_hot_dot(a, b, contract=((1,), (0,))):
    return dot(a, b, contract).astype(bf16)


def iota(shape, dim):
    return lax.broadcasted_iota(jnp.int32, shape, dim)


def to_segments():
    n = EXPERTS * SEG
    r, q = iota((n, n), 0), iota((n, n), 1)
    return (q == (r & (SEG - 1)) * EXPERTS + (r >> 3)).astype(f32).astype(bf16)


def from_segments():
    n = EXPERTS * SEG
    q, r = iota((n, n), 0), iota((n, n), 1)
    return (r == (q & (EXPERTS - 1)) * SEG + (q >> 6)).astype(f32).astype(bf16)


def slot_masks(routes_ref, start, tokens):
    own = routes_ref[:, pl.ds(start, tokens)]
    e = iota((EXPERTS, tokens), 0)
    first = (own[0:1, :] == e).astype(f32)
    second = (own[1:2, :] == e).astype(f32)
    before = (iota((tokens, tokens), 0) < iota((tokens, tokens), 1)).astype(f32)
    count = dot((first + second).astype(bf16), before.astype(bf16))
    return first, second, count


def attention_kernel(user_ref, sp_ref, stream, base, *refs):
    keys, values, adapters = refs[0:4], refs[4:8], refs[8:12]
    gain_a, gain_e, routes = refs[12:15]
    n_out = 1 + len(CHUNKS)
    hidden = refs[15]
    sends = refs[16 : 15 + n_out]
    xn, query, stack = refs[15 + n_out :]
    tokens = stream.shape[0]
    me = sp_ref[0]

    total = jnp.zeros((tokens, 1), f32)
    for s in range(SEG):
        x = stream[:, s * WIDE : (s + 1) * WIDE].astype(f32)
        total += jnp.sum(x * x, axis=1, keepdims=True)
    scale = lax.rsqrt(total * (1.0 / D) + epsilon)
    for s in range(SEG):
        cols = slice(s * WIDE, (s + 1) * WIDE)
        xn[:, cols] = (
            stream[:, cols].astype(f32) * scale * gain_a[:, cols].astype(f32)
        ).astype(bf16)

    quarter = D // 4
    starts = [
        pl.multiple_of(((me + shift) & 3) * quarter, quarter) for shift in (0, 3, 1, 2)
    ]
    low = jnp.zeros((tokens, RANK), f32)
    for start, part in zip(starts, adapters):
        low += dot(xn[:, pl.ds(start, quarter)], part[0:RANK, :], ((1,), (1,)))
    low = low.astype(bf16)
    for start, part in zip(starts, adapters):
        cols = pl.ds(start, quarter)
        delta = dot(low, part[RANK : 2 * RANK, :])
        query[:, cols] = (base[:, cols].astype(f32) + delta).astype(bf16)

    group = HEADS // KV_HEADS
    total = jnp.zeros((tokens, 1), f32)
    for g in range(KV_HEADS):
        kv = slice(g * HEAD, (g + 1) * HEAD)
        q = jnp.concatenate(
            [query[:, (g * group + h) * HEAD : (g * group + h + 1) * HEAD] for h in range(group)],
            axis=0,
        )
        k = jnp.concatenate([r[:, kv] for r in keys], axis=0)
        v = jnp.concatenate([r[:, kv] for r in values], axis=0)
        scores = dot(q, k, ((1,), (1,))) * HEAD ** (-0.5)
        e = jnp.exp(scores - jnp.max(scores, axis=1, keepdims=True))
        p = (e * (1.0 / jnp.sum(e, axis=1, keepdims=True))).astype(bf16)
        o = dot(p, v)
        for h in range(group):
            cols = slice((g * group + h) * HEAD, (g * group + h + 1) * HEAD)
            state = (
                stream[:, cols].astype(f32) + o[h * tokens : (h + 1) * tokens, :]
            ).astype(bf16)
            hidden[:, cols] = state
            wide = state.astype(f32)
            total += jnp.sum(wide * wide, axis=1, keepdims=True)

    scale = lax.rsqrt(total * (1.0 / D) + epsilon)
    first, second, count = slot_masks(routes, pl.multiple_of(me * tokens, tokens), tokens)
    named = first + second
    pick = jnp.concatenate(
        [jnp.where(count == c, named, 0.0) for c in range(SLOTS)], axis=0
    ).astype(bf16)
    for s in range(SEG):
        cols = slice(s * WIDE, (s + 1) * WIDE)
        hn = (hidden[:, cols].astype(f32) * scale * gain_e[:, cols].astype(f32)).astype(bf16)
        rows = one_hot_dot(pick, hn)
        for c in range(SLOTS):
            stack[s * EXPERTS : (s + 1) * EXPERTS, c * WIDE : (c + 1) * WIDE] = rows[
                c * EXPERTS : (c + 1) * EXPERTS, :
            ]
    order = to_segments()
    c = 0
    for n, send in zip(CHUNKS, sends):
        send[...] = one_hot_dot(order, stack[:, c * WIDE : (c + n) * WIDE])
        c += n


def attention(user, sp, stream, base, keys, values, adapters, gain_a, gain_e, routes):
    tokens = stream.shape[0]
    outs = [jax.ShapeDtypeStruct((tokens, D), bf16)] + [
        jax.ShapeDtypeStruct((EXPERTS * SEG, n * WIDE), bf16) for n in CHUNKS
    ]
    return pl.pallas_call(
        attention_kernel,
        out_shape=outs,
        in_specs=[SMEM_SPEC] * 2 + [VMEM_SPEC] * 17,
        out_specs=[VMEM_SPEC] * len(outs),
        scratch_shapes=[
            pltpu.VMEM((tokens, D), bf16),
            pltpu.VMEM((tokens, D), bf16),
            pltpu.VMEM((EXPERTS * SEG, SLOTS * WIDE), bf16),
        ],
        compiler_params=PARAMS,
        name="attention",
    )(user, sp, stream, base, *keys, *values, *adapters, gain_a, gain_e, routes)


def arrive_kernel(n, received, out):
    rows = one_hot_dot(from_segments(), received[...])
    for c in range(n):
        for s in range(SEG):
            out[c * EXPERTS : (c + 1) * EXPERTS, s * WIDE : (s + 1) * WIDE] = rows[
                s * EXPERTS : (s + 1) * EXPERTS, c * WIDE : (c + 1) * WIDE
            ]


def arrive(n, received):
    return pl.pallas_call(
        functools.partial(arrive_kernel, n),
        out_shape=jax.ShapeDtypeStruct((n * EXPERTS, D), bf16),
        in_specs=[VMEM_SPEC],
        out_specs=VMEM_SPEC,
        compiler_params=PARAMS,
        name="arrive",
    )(received)


def leave_kernel(n, own, other, last, out, stack):
    for c in range(n):
        for s in range(SEG):
            at = slice(c * EXPERTS, (c + 1) * EXPERTS), slice(s * WIDE, (s + 1) * WIDE)
            total = own[at].astype(f32) + other[at].astype(f32) + last[at].astype(f32)
            stack[s * EXPERTS : (s + 1) * EXPERTS, c * WIDE : (c + 1) * WIDE] = total.astype(bf16)
    out[...] = one_hot_dot(to_segments(), stack[...])


def leave(n, *terms):
    shape = (EXPERTS * SEG, n * WIDE)
    return pl.pallas_call(
        functools.partial(leave_kernel, n),
        out_shape=jax.ShapeDtypeStruct(shape, bf16),
        in_specs=[VMEM_SPEC] * 3,
        out_specs=VMEM_SPEC,
        scratch_shapes=[pltpu.VMEM(shape, bf16)],
        compiler_params=PARAMS,
        name="leave",
    )(*terms)


STEPS = 4


def expert_kernel(n, *refs):
    rows, (gate, up, down) = refs[0:n], refs[n : n + 3]
    outs = refs[n + 3 : 2 * n + 3]
    gate_sum, up_sum, act = refs[2 * n + 3 :]
    i = pl.program_id(0)

    @pl.when(i == 0)
    def _():
        gate_sum[...] = jnp.zeros_like(gate_sum)
        up_sum[...] = jnp.zeros_like(up_sum)

    @pl.when(i < STEPS)
    def _():
        x = jnp.concatenate([r[...] for r in rows], axis=0)
        gate_sum[...] += dot(x, gate[...])
        up_sum[...] += dot(x, up[...])

    @pl.when(i == STEPS - 1)
    def _():
        v = gate_sum[...]
        act[...] = (v / (1.0 + jnp.exp(-v)) * up_sum[...]).astype(bf16)

    @pl.when(i >= STEPS)
    def _():
        part = dot(act[...], down[...]).astype(bf16)
        size = rows[0].shape[0]
        for k in range(n):
            outs[k][...] = part[k * size : (k + 1) * size, :]


def expert(pieces, gate, up, down):
    n, size, hidden = len(pieces), pieces[0].shape[0], gate.shape[1]
    depth = D // STEPS
    first = lambda i: (jnp.minimum(i, STEPS - 1), 0)
    last = lambda i: (0, jnp.maximum(i - STEPS, 0))
    flops = 6 * n * size * D * hidden
    return pl.pallas_call(
        functools.partial(expert_kernel, n),
        out_shape=[jax.ShapeDtypeStruct((size, D), bf16)] * n,
        grid=(2 * STEPS,),
        in_specs=[pl.BlockSpec((size, depth), lambda i: (0, jnp.minimum(i, STEPS - 1)))] * n
        + [pl.BlockSpec((depth, hidden), first)] * 2
        + [pl.BlockSpec((hidden, depth), last)],
        out_specs=[pl.BlockSpec((size, depth), last)] * n,
        scratch_shapes=[
            pltpu.VMEM((n * size, hidden), f32),
            pltpu.VMEM((n * size, hidden), f32),
            pltpu.VMEM((n * size, hidden), bf16),
        ],
        compiler_params=PARAMS,
        cost_estimate=pl.CostEstimate(
            flops=flops,
            transcendentals=n * size * hidden,
            bytes_accessed=6 * D * hidden + 4 * n * size * D,
        ),
        name="expert",
    )(*pieces, gate, up, down)


def combine_kernel(sp_ref, routes, weights, *refs):
    received, out, stack = refs[: len(CHUNKS)], refs[-2], refs[-1]
    tokens = out.shape[0]
    first, second, count = slot_masks(routes, pl.multiple_of(sp_ref[0] * tokens, tokens), tokens)
    w = weights[...].astype(f32)
    w = w / jnp.sum(w, axis=0, keepdims=True)
    share = first * w[0:1, :] + second * w[1:2, :]
    share = jnp.concatenate(
        [jnp.where(count == c, share, 0.0) for c in range(SLOTS)], axis=0
    )
    high = share.astype(bf16)
    rest = (share - high.astype(f32)).astype(bf16)
    order = from_segments()
    c = 0
    for n, r in zip(CHUNKS, received):
        stack[:, c * WIDE : (c + n) * WIDE] = one_hot_dot(order, r[...])
        c += n
    for s in range(SEG):
        rows = jnp.concatenate(
            [
                stack[s * EXPERTS : (s + 1) * EXPERTS, k * WIDE : (k + 1) * WIDE]
                for k in range(SLOTS)
            ],
            axis=0,
        )
        both = dot(high, rows, ((0,), (0,))) + dot(rest, rows, ((0,), (0,)))
        out[:, s * WIDE : (s + 1) * WIDE] = both.astype(bf16)


def combine(sp, routes, weights, received, tokens):
    return pl.pallas_call(
        combine_kernel,
        out_shape=jax.ShapeDtypeStruct((tokens, D), bf16),
        in_specs=[SMEM_SPEC] + [VMEM_SPEC] * (2 + len(received)),
        out_specs=VMEM_SPEC,
        scratch_shapes=[pltpu.VMEM((EXPERTS * SEG, SLOTS * WIDE), bf16)],
        compiler_params=PARAMS,
        name="combine",
    )(sp, routes, weights, *received)


def right(x):
    return lax.ppermute(x, "sp", [(i, (i + 1) % 4) for i in range(4)])


def left(x):
    return lax.ppermute(x, "sp", [(i, (i + 3) % 4) for i in range(4)])


def across(x):
    return lax.ppermute(x, "sp", [(i, (i + 2) % 4) for i in range(4)])


def exchange(x, n):
    cut = x.reshape(EXPERTS, SEG, n * WIDE)
    moved = lax.all_to_all(cut, "ep", split_axis=0, concat_axis=0, tiled=True)
    return moved.reshape(EXPERTS * SEG, n * WIDE)


def after(x, *others):
    return lax.optimization_barrier((x, *others))[0]


def feed_forward(sends, gate, up, down):
    count = len(CHUNKS)
    first = exchange(sends[0], CHUNKS[0])
    second = exchange(after(sends[1], first), CHUNKS[1])
    arrived = [first, second]
    ways = [(right, left) if c % 2 == 0 else (left, right) for c in range(count)]
    pieces, parts = [], []
    for c, n in enumerate(CHUNKS):
        ahead, back = ways[c]
        x = arrived[c]
        if c == 0:
            own = arrive(n, x)
            behind, front, far = ahead(own), back(own), across(own)
        else:
            _, _, front_before, far_before = pieces[-1]
            own = arrive(n, x if c == 1 else after(x, parts[-1][0]))
            behind = ahead(own if c == 1 else after(own, front_before))
            front = back(own if c == 1 else after(own, far_before))
            parts.append(expert(pieces[-1], gate, up, down))
            far = ahead(after(behind, parts[-1][0]) if c == 1 else behind)
        pieces.append((own, behind, front, far))
        if c + 2 < count:
            ready = after(sends[c + 2], arrived[c + 1], behind, front, far)
            arrived.append(exchange(ready, CHUNKS[c + 2]))
    parts.append(expert(pieces[-1], gate, up, down))
    returned, done = [], None
    for c, n in enumerate(CHUNKS):
        ahead, back = ways[c]
        p_own, p_behind, p_front, p_far = parts[c]
        if c + 1 < count:
            p_far = after(p_far, pieces[c + 1][1])
        passed = back(p_far)
        whole = (p_behind.astype(f32) + passed.astype(f32)).astype(bf16)
        out = leave(n, p_own, ahead(p_front), back(whole))
        done = exchange(out if done is None else after(out, done), n)
        returned.append(done)
    return returned


def on_device(
    stream,
    query_base,
    key_heads,
    value_heads,
    attention_gain,
    expert_gain,
    adapter_down,
    adapter_up,
    user_index,
    routes,
    route_weights,
    gate_weight,
    up_weight,
    down_weight,
):
    sp = lax.axis_index("sp").astype(jnp.int32).reshape(1)
    columns = user_index[0] * RANK + jnp.arange(RANK, dtype=jnp.int32)
    select = (columns[:, None] == jnp.arange(4 * RANK, dtype=jnp.int32)[None, :]).astype(bf16)
    adapter = jnp.concatenate(
        [
            one_hot_dot(select, adapter_down, ((1,), (1,))),
            one_hot_dot(select, adapter_up, ((1,), (1,))),
        ],
        axis=0,
    )
    k_left, k_right = right(key_heads), left(key_heads)
    v_left, v_right = right(value_heads), left(value_heads)
    d_left, d_right = right(adapter), left(adapter)
    keys = (key_heads, k_left, k_right, right(k_left))
    values = (value_heads, v_left, v_right, left(v_right))
    adapters = (adapter, d_left, d_right, right(d_left))
    routes_t, weights_t = routes.T, route_weights.T
    hidden, *sends = attention(
        user_index,
        sp,
        stream,
        query_base,
        keys,
        values,
        adapters,
        attention_gain.reshape(1, D),
        expert_gain.reshape(1, D),
        routes_t,
    )
    gate, up, down = gate_weight[0], up_weight[0], down_weight[0]
    received = feed_forward(sends, gate, up, down)
    moe_out = combine(sp, routes_t, weights_t, received, stream.shape[0])
    return (hidden, moe_out)


def solution(mesh):
    in_specs = (
        P(("ep", "sp"), None),
        P(("ep", "sp"), None),
        P(("ep", "sp"), None),
        P(("ep", "sp"), None),
        P(),
        P(),
        P("sp", None),
        P("sp", None),
        P("ep"),
        P("ep", None),
        P(("ep", "sp"), None),
        P("ep", None, "sp"),
        P("ep", None, "sp"),
        P("ep", "sp", None),
    )
    out_specs = (P(("ep", "sp"), None), P(("ep", "sp"), None))
    return jax.shard_map(
        on_device, mesh=mesh, in_specs=in_specs, out_specs=out_specs, check_vma=False
    )
```

```python
import functools

import jax
import jax.numpy as jnp
from jax import lax
from jax.experimental import pallas as pl
from jax.experimental.pallas import tpu as pltpu
from jax.sharding import PartitionSpec as P

D = 4096
HEADS = 32
KV_HEADS = 8
HEAD = 128
RANK = 32
SLOTS = 5
SEG = 8
WIDE = D // SEG
EXPERTS = 64
CHUNKS = (1, 2, 2)

epsilon = 1e-06
bf16 = jnp.bfloat16
f32 = jnp.float32
VMEM_SPEC = pl.BlockSpec(memory_space=pltpu.VMEM)
SMEM_SPEC = pl.BlockSpec(memory_space=pltpu.SMEM)
PARAMS = pltpu.CompilerParams(vmem_limit_bytes=56 << 20)


def dot(a, b, contract=((1,), (0,))):
    return lax.dot_general(a, b, (contract, ((), ())), preferred_element_type=f32)


def one_hot_dot(a, b, contract=((1,), (0,))):
    return dot(a, b, contract).astype(bf16)


def iota(shape, dim):
    return lax.broadcasted_iota(jnp.int32, shape, dim)


def to_segments():
    n = EXPERTS * SEG
    r, q = iota((n, n), 0), iota((n, n), 1)
    return (q == (r & (SEG - 1)) * EXPERTS + (r >> 3)).astype(f32).astype(bf16)


def from_segments():
    n = EXPERTS * SEG
    q, r = iota((n, n), 0), iota((n, n), 1)
    return (r == (q & (EXPERTS - 1)) * SEG + (q >> 6)).astype(f32).astype(bf16)


def slot_masks(routes_ref, start, tokens):
    own = routes_ref[:, pl.ds(start, tokens)]
    e = iota((EXPERTS, tokens), 0)
    first = (own[0:1, :] == e).astype(f32)
    second = (own[1:2, :] == e).astype(f32)
    before = (iota((tokens, tokens), 0) < iota((tokens, tokens), 1)).astype(f32)
    count = dot((first + second).astype(bf16), before.astype(bf16))
    return first, second, count


def attention_kernel(user_ref, sp_ref, stream, base, *refs):
    keys, values, adapters = refs[0:4], refs[4:8], refs[8:12]
    gain_a, gain_e, routes = refs[12:15]
    n_out = 1 + len(CHUNKS)
    hidden = refs[15]
    sends = refs[16 : 15 + n_out]
    xn, query, stack = refs[15 + n_out :]
    tokens = stream.shape[0]
    me = sp_ref[0]

    total = jnp.zeros((tokens, 1), f32)
    for s in range(SEG):
        x = stream[:, s * WIDE : (s + 1) * WIDE].astype(f32)
        total += jnp.sum(x * x, axis=1, keepdims=True)
    scale = lax.rsqrt(total * (1.0 / D) + epsilon)
    for s in range(SEG):
        cols = slice(s * WIDE, (s + 1) * WIDE)
        xn[:, cols] = (
            stream[:, cols].astype(f32) * scale * gain_a[:, cols].astype(f32)
        ).astype(bf16)

    quarter = D // 4
    starts = [
        pl.multiple_of(((me + shift) & 3) * quarter, quarter) for shift in (0, 3, 1, 2)
    ]
    low = jnp.zeros((tokens, RANK), f32)
    for start, part in zip(starts, adapters):
        low += dot(xn[:, pl.ds(start, quarter)], part[0:RANK, :], ((1,), (1,)))
    low = low.astype(bf16)
    for start, part in zip(starts, adapters):
        cols = pl.ds(start, quarter)
        delta = dot(low, part[RANK : 2 * RANK, :])
        query[:, cols] = (base[:, cols].astype(f32) + delta).astype(bf16)

    group = HEADS // KV_HEADS
    total = jnp.zeros((tokens, 1), f32)
    for g in range(KV_HEADS):
        kv = slice(g * HEAD, (g + 1) * HEAD)
        q = jnp.concatenate(
            [query[:, (g * group + h) * HEAD : (g * group + h + 1) * HEAD] for h in range(group)],
            axis=0,
        )
        k = jnp.concatenate([r[:, kv] for r in keys], axis=0)
        v = jnp.concatenate([r[:, kv] for r in values], axis=0)
        scores = dot(q, k, ((1,), (1,))) * HEAD ** (-0.5)
        e = jnp.exp(scores - jnp.max(scores, axis=1, keepdims=True))
        p = (e * (1.0 / jnp.sum(e, axis=1, keepdims=True))).astype(bf16)
        o = dot(p, v)
        for h in range(group):
            cols = slice((g * group + h) * HEAD, (g * group + h + 1) * HEAD)
            state = (
                stream[:, cols].astype(f32) + o[h * tokens : (h + 1) * tokens, :]
            ).astype(bf16)
            hidden[:, cols] = state
            wide = state.astype(f32)
            total += jnp.sum(wide * wide, axis=1, keepdims=True)

    scale = lax.rsqrt(total * (1.0 / D) + epsilon)
    first, second, count = slot_masks(routes, pl.multiple_of(me * tokens, tokens), tokens)
    named = first + second
    pick = jnp.concatenate(
        [jnp.where(count == c, named, 0.0) for c in range(SLOTS)], axis=0
    ).astype(bf16)
    for s in range(SEG):
        cols = slice(s * WIDE, (s + 1) * WIDE)
        hn = (hidden[:, cols].astype(f32) * scale * gain_e[:, cols].astype(f32)).astype(bf16)
        rows = one_hot_dot(pick, hn)
        for c in range(SLOTS):
            stack[s * EXPERTS : (s + 1) * EXPERTS, c * WIDE : (c + 1) * WIDE] = rows[
                c * EXPERTS : (c + 1) * EXPERTS, :
            ]
    order = to_segments()
    c = 0
    for n, send in zip(CHUNKS, sends):
        send[...] = one_hot_dot(order, stack[:, c * WIDE : (c + n) * WIDE])
        c += n


def attention(user, sp, stream, base, keys, values, adapters, gain_a, gain_e, routes):
    tokens = stream.shape[0]
    outs = [jax.ShapeDtypeStruct((tokens, D), bf16)] + [
        jax.ShapeDtypeStruct((EXPERTS * SEG, n * WIDE), bf16) for n in CHUNKS
    ]
    return pl.pallas_call(
        attention_kernel,
        out_shape=outs,
        in_specs=[SMEM_SPEC] * 2 + [VMEM_SPEC] * 17,
        out_specs=[VMEM_SPEC] * len(outs),
        scratch_shapes=[
            pltpu.VMEM((tokens, D), bf16),
            pltpu.VMEM((tokens, D), bf16),
            pltpu.VMEM((EXPERTS * SEG, SLOTS * WIDE), bf16),
        ],
        compiler_params=PARAMS,
        name="attention",
    )(user, sp, stream, base, *keys, *values, *adapters, gain_a, gain_e, routes)


def arrive_kernel(n, received, out):
    rows = one_hot_dot(from_segments(), received[...])
    for c in range(n):
        for s in range(SEG):
            out[c * EXPERTS : (c + 1) * EXPERTS, s * WIDE : (s + 1) * WIDE] = rows[
                s * EXPERTS : (s + 1) * EXPERTS, c * WIDE : (c + 1) * WIDE
            ]


def arrive(n, received):
    return pl.pallas_call(
        functools.partial(arrive_kernel, n),
        out_shape=jax.ShapeDtypeStruct((n * EXPERTS, D), bf16),
        in_specs=[VMEM_SPEC],
        out_specs=VMEM_SPEC,
        compiler_params=PARAMS,
        name="arrive",
    )(received)


def leave_kernel(n, own, other, last, out, stack):
    for c in range(n):
        for s in range(SEG):
            at = slice(c * EXPERTS, (c + 1) * EXPERTS), slice(s * WIDE, (s + 1) * WIDE)
            total = own[at].astype(f32) + other[at].astype(f32) + last[at].astype(f32)
            stack[s * EXPERTS : (s + 1) * EXPERTS, c * WIDE : (c + 1) * WIDE] = total.astype(bf16)
    out[...] = one_hot_dot(to_segments(), stack[...])


def leave(n, *terms):
    shape = (EXPERTS * SEG, n * WIDE)
    return pl.pallas_call(
        functools.partial(leave_kernel, n),
        out_shape=jax.ShapeDtypeStruct(shape, bf16),
        in_specs=[VMEM_SPEC] * 3,
        out_specs=VMEM_SPEC,
        scratch_shapes=[pltpu.VMEM(shape, bf16)],
        compiler_params=PARAMS,
        name="leave",
    )(*terms)


STEPS = 2


def expert_kernel(n, *refs):
    rows, (gate, up, down) = refs[0:n], refs[n : n + 3]
    outs = refs[n + 3 : 2 * n + 3]
    gate_sum, up_sum, act = refs[2 * n + 3 :]
    i = pl.program_id(0)

    @pl.when(i == 0)
    def _():
        gate_sum[...] = jnp.zeros_like(gate_sum)
        up_sum[...] = jnp.zeros_like(up_sum)

    @pl.when(i < STEPS)
    def _():
        x = jnp.concatenate([r[...] for r in rows], axis=0)
        gate_sum[...] += dot(x, gate[...])
        up_sum[...] += dot(x, up[...])

    @pl.when(i == STEPS - 1)
    def _():
        v = gate_sum[...]
        act[...] = (v / (1.0 + jnp.exp(-v)) * up_sum[...]).astype(bf16)

    @pl.when(i >= STEPS)
    def _():
        part = dot(act[...], down[...]).astype(bf16)
        size = rows[0].shape[0]
        for k in range(n):
            outs[k][...] = part[k * size : (k + 1) * size, :]


def expert(pieces, gate, up, down):
    n, size, hidden = len(pieces), pieces[0].shape[0], gate.shape[1]
    depth = D // STEPS
    first = lambda i: (jnp.minimum(i, STEPS - 1), 0)
    last = lambda i: (0, jnp.maximum(i - STEPS, 0))
    flops = 6 * n * size * D * hidden
    return pl.pallas_call(
        functools.partial(expert_kernel, n),
        out_shape=[jax.ShapeDtypeStruct((size, D), bf16)] * n,
        grid=(2 * STEPS,),
        in_specs=[pl.BlockSpec((size, depth), lambda i: (0, jnp.minimum(i, STEPS - 1)))] * n
        + [pl.BlockSpec((depth, hidden), first)] * 2
        + [pl.BlockSpec((hidden, depth), last)],
        out_specs=[pl.BlockSpec((size, depth), last)] * n,
        scratch_shapes=[
            pltpu.VMEM((n * size, hidden), f32),
            pltpu.VMEM((n * size, hidden), f32),
            pltpu.VMEM((n * size, hidden), bf16),
        ],
        compiler_params=PARAMS,
        cost_estimate=pl.CostEstimate(
            flops=flops,
            transcendentals=n * size * hidden,
            bytes_accessed=6 * D * hidden + 4 * n * size * D,
        ),
        name="expert",
    )(*pieces, gate, up, down)


def combine_kernel(sp_ref, routes, weights, *refs):
    received, out, stack = refs[: len(CHUNKS)], refs[-2], refs[-1]
    tokens = out.shape[0]
    first, second, count = slot_masks(routes, pl.multiple_of(sp_ref[0] * tokens, tokens), tokens)
    w = weights[...].astype(f32)
    w = w / jnp.sum(w, axis=0, keepdims=True)
    share = first * w[0:1, :] + second * w[1:2, :]
    share = jnp.concatenate(
        [jnp.where(count == c, share, 0.0) for c in range(SLOTS)], axis=0
    )
    high = share.astype(bf16)
    rest = (share - high.astype(f32)).astype(bf16)
    order = from_segments()
    c = 0
    for n, r in zip(CHUNKS, received):
        stack[:, c * WIDE : (c + n) * WIDE] = one_hot_dot(order, r[...])
        c += n
    for s in range(SEG):
        rows = jnp.concatenate(
            [
                stack[s * EXPERTS : (s + 1) * EXPERTS, k * WIDE : (k + 1) * WIDE]
                for k in range(SLOTS)
            ],
            axis=0,
        )
        both = dot(high, rows, ((0,), (0,))) + dot(rest, rows, ((0,), (0,)))
        out[:, s * WIDE : (s + 1) * WIDE] = both.astype(bf16)


def combine(sp, routes, weights, received, tokens):
    return pl.pallas_call(
        combine_kernel,
        out_shape=jax.ShapeDtypeStruct((tokens, D), bf16),
        in_specs=[SMEM_SPEC] + [VMEM_SPEC] * (2 + len(received)),
        out_specs=VMEM_SPEC,
        scratch_shapes=[pltpu.VMEM((EXPERTS * SEG, SLOTS * WIDE), bf16)],
        compiler_params=PARAMS,
        name="combine",
    )(sp, routes, weights, *received)


def right(x):
    return lax.ppermute(x, "sp", [(i, (i + 1) % 4) for i in range(4)])


def left(x):
    return lax.ppermute(x, "sp", [(i, (i + 3) % 4) for i in range(4)])


def across(x):
    return lax.ppermute(x, "sp", [(i, (i + 2) % 4) for i in range(4)])


def exchange(x, n):
    cut = x.reshape(EXPERTS, SEG, n * WIDE)
    moved = lax.all_to_all(cut, "ep", split_axis=0, concat_axis=0, tiled=True)
    return moved.reshape(EXPERTS * SEG, n * WIDE)


def after(x, *others):
    return lax.optimization_barrier((x, *others))[0]


def feed_forward(sends, gate, up, down):
    count = len(CHUNKS)
    first = exchange(sends[0], CHUNKS[0])
    second = exchange(after(sends[1], first), CHUNKS[1])
    arrived = [first, second]
    ways = [(right, left) if c % 2 == 0 else (left, right) for c in range(count)]
    pieces, parts = [], []
    for c, n in enumerate(CHUNKS):
        ahead, back = ways[c]
        x = arrived[c]
        if c == 0:
            own = arrive(n, x)
            behind, front, far = ahead(own), back(own), across(own)
        else:
            _, _, front_before, far_before = pieces[-1]
            own = arrive(n, x if c == 1 else after(x, parts[-1][0]))
            behind = ahead(own if c == 1 else after(own, front_before))
            front = back(own if c == 1 else after(own, far_before))
            parts.append(expert(pieces[-1], gate, up, down))
            far = ahead(after(behind, parts[-1][0]) if c == 1 else behind)
        pieces.append((own, behind, front, far))
        if c + 2 < count:
            ready = after(sends[c + 2], arrived[c + 1], behind, front, far)
            arrived.append(exchange(ready, CHUNKS[c + 2]))
    parts.append(expert(pieces[-1], gate, up, down))
    returned, done = [], None
    for c, n in enumerate(CHUNKS):
        ahead, back = ways[c]
        p_own, p_behind, p_front, p_far = parts[c]
        if c + 1 < count:
            p_far = after(p_far, pieces[c + 1][1])
        passed = back(p_far)
        whole = (p_behind.astype(f32) + passed.astype(f32)).astype(bf16)
        out = leave(n, p_own, ahead(p_front), back(whole))
        done = exchange(out if done is None else after(out, done), n)
        returned.append(done)
    return returned


def on_device(
    stream,
    query_base,
    key_heads,
    value_heads,
    attention_gain,
    expert_gain,
    adapter_down,
    adapter_up,
    user_index,
    routes,
    route_weights,
    gate_weight,
    up_weight,
    down_weight,
):
    sp = lax.axis_index("sp").astype(jnp.int32).reshape(1)
    columns = user_index[0] * RANK + jnp.arange(RANK, dtype=jnp.int32)
    select = (columns[:, None] == jnp.arange(4 * RANK, dtype=jnp.int32)[None, :]).astype(bf16)
    adapter = jnp.concatenate(
        [
            one_hot_dot(select, adapter_down, ((1,), (1,))),
            one_hot_dot(select, adapter_up, ((1,), (1,))),
        ],
        axis=0,
    )
    k_left, k_right = right(key_heads), left(key_heads)
    v_left, v_right = right(value_heads), left(value_heads)
    d_left, d_right = right(adapter), left(adapter)
    keys = (key_heads, k_left, k_right, right(k_left))
    values = (value_heads, v_left, v_right, left(v_right))
    adapters = (adapter, d_left, d_right, right(d_left))
    routes_t, weights_t = routes.T, route_weights.T
    hidden, *sends = attention(
        user_index,
        sp,
        stream,
        query_base,
        keys,
        values,
        adapters,
        attention_gain.reshape(1, D),
        expert_gain.reshape(1, D),
        routes_t,
    )
    gate, up, down = gate_weight[0], up_weight[0], down_weight[0]
    received = feed_forward(sends, gate, up, down)
    moe_out = combine(sp, routes_t, weights_t, received, stream.shape[0])
    return (hidden, moe_out)


def solution(mesh):
    in_specs = (
        P(("ep", "sp"), None),
        P(("ep", "sp"), None),
        P(("ep", "sp"), None),
        P(("ep", "sp"), None),
        P(),
        P(),
        P("sp", None),
        P("sp", None),
        P("ep"),
        P("ep", None),
        P(("ep", "sp"), None),
        P("ep", None, "sp"),
        P("ep", None, "sp"),
        P("ep", "sp", None),
    )
    out_specs = (P(("ep", "sp"), None), P(("ep", "sp"), None))
    return jax.shard_map(
        on_device, mesh=mesh, in_specs=in_specs, out_specs=out_specs, check_vma=False
    )
```
